128 devices in a mesh: wrap: 16 (over y_hi, x, core), span: 8 (over z, y_lo).
Axes of the slice: x: 4, y: 4 (y_hi: 2, y_lo: 2; y = y_hi * 2 + y_lo), z: 4, core: 2. Of those that a mesh axis runs over, the one named last changes fastest.
Arguments:
- density: float32 [256, 16, 1024], P('wrap', None, 'span'), may hold values from 0.8 to 1.2
- velocity: float32 [3, 256, 16, 1024], P(None, 'wrap', None, 'span'), may hold values from -0.4 to 0.4
- pressure: float32 [256, 16, 1024], P('wrap', None, 'span'), may hold values from 0.7 to 1.4
- metrics: float32 [9, 256, 16, 1024], P(None, 'wrap', None, 'span'), may hold values from -0.3 to 0.3
- volume: float32 [256, 16, 1024], P('wrap', None, 'span'), may hold values from 0.5 to 2
- wake_partner: int32 [256], P('wrap'), may hold values from 0 to 255, as said below
- iblank: int32 [256, 16, 1024], P('wrap', None, 'span'), may hold values 0 or 1
Outputs:
- final_state: float32 [5, 256, 16, 1024], P(None, 'wrap', None, 'span')
The draws below stay inside these ranges and needn't reach their ends.
Inputs may be any that keep to these rules, and one draw needn't show every extreme that they name: For i in i-slab s (rows s * 16 to (s + 1) * 16 - 1, s from 0), wake_partner[i] is one of the rows (n - 1 - s) * 16 to (n - s) * 16 - 1 with n = 16; each of those rows is named once.
All inputs are finite; a program needn't handle non-finite values. No bound on the sum of `iblank` on one device may be relied on, other than what follows from the above.
Results may differ from the reference program's by a relative error of at most 0.0003.
Values sent between devices are 32-bit elements; how exact they have to be, the bound alone decides.
A program may use at most 64 MiB of HBM per device.

```python
import math
import jax
import jax.numpy as jnp
from jax import lax

CI = 16
J = 16
CK = 128
NI = 256
NK = 1024


def draw_wake_partner(key, part):
    slabs = NI // CI
    slab_keys = jax.random.split(key, slabs)
    shuffled = jax.vmap(lambda one_key: jax.random.permutation(one_key, CI))(slab_keys).astype(jnp.int32)
    mirror_start = (slabs - 1 - jnp.arange(slabs, dtype=jnp.int32))[:, None] * CI
    return (mirror_start + shuffled).reshape(NI).astype(jnp.int32)


def with_ends(drawn, own_key, least, high):
    spot = [jax.random.randint(jax.random.fold_in(own_key, axis), (), 0, length) for axis, length in enumerate(drawn.shape)]
    widest = drawn.shape.index(max(drawn.shape))
    beside = spot[:widest] + [(spot[widest] + 1) % drawn.shape[widest]] + spot[widest + 1:]
    return drawn.at[tuple(spot)].set(least).at[tuple(beside)].set(high)


def block_levels(stream_key, extent, cuts, smallest, largest):
    level, own = 1.0, jax.random.fold_in(stream_key, 6)
    for dim, shards_of in cuts:
        steps = jnp.exp(jax.random.uniform(jax.random.fold_in(own, dim), (shards_of,), jnp.float32, smallest / len(cuts), largest / len(cuts)))
        level = level * jnp.repeat(steps, extent[dim] // shards_of).reshape([-1 if axis == dim else 1 for axis in range(len(extent))])
    return level


def setup_inputs(seed: int = 0) -> dict:
    keys = jax.random.split(jax.random.key(seed), 8)
    density = jnp.clip(0.8 + 0.40000004 * jax.random.uniform(keys[0], (NI, J, NK), jnp.float32) ** block_levels(keys[0], (NI, J, NK), ((0, 16), (2, 8)), -0.2, 0.2), 0.8, 1.2)
    velocity = jnp.clip(jax.random.uniform(keys[1], (3, NI, J, NK), jnp.float32, -0.4, 0.4) * block_levels(keys[1], (3, NI, J, NK), ((1, 16), (3, 8)), -0.4, 0.0), -0.4, 0.4)
    pressure = jnp.clip(0.7 + 0.7 * jax.random.uniform(keys[2], (NI, J, NK), jnp.float32) ** block_levels(keys[2], (NI, J, NK), ((0, 16), (2, 8)), -0.2, 0.2), 0.7, 1.4)
    metrics = jnp.clip(jax.random.uniform(keys[3], (9, NI, J, NK), jnp.float32, -0.3, 0.3) * block_levels(keys[3], (9, NI, J, NK), ((1, 16), (3, 8)), -0.4, 0.0), -0.3, 0.3)
    volume = jnp.clip(jnp.exp(math.log(2.0) - 1.3862944 * jax.random.uniform(keys[4], (NI, J, NK), jnp.float32) ** block_levels(keys[4], (NI, J, NK), ((0, 16), (2, 8)), -0.2, 0.2)), 0.5, 2.0)
    wake_partner = draw_wake_partner(jax.random.fold_in(keys[7], 71), 0)
    iblank = with_ends((jax.random.randint(keys[6], (NI, J, NK), 0, 8) < 7).astype(jnp.int32), jax.random.fold_in(keys[6], 1), 0, 1)
    return {"density": density, "velocity": velocity, "pressure": pressure, "metrics": metrics, "volume": volume, "wake_partner": wake_partner, "iblank": iblank}


epsilon = 1e-06
viscosity = 0.8
conduction = 1.0
time_step = 0.05

def window(array, start, length, array_dim):
    return lax.slice_in_dim(array, start, start + length, axis=array_dim)

def reconstruct(first, second, third, fourth, fifth):
    guess_left = (2.0 * first - 7.0 * second + 11.0 * third) / 6.0
    guess_mid = (-second + 5.0 * third + 2.0 * fourth) / 6.0
    guess_right = (2.0 * third + 5.0 * fourth - fifth) / 6.0
    smooth_left = 13.0 / 12.0 * (first - 2.0 * second + third) ** 2 + 0.25 * (first - 4.0 * second + 3.0 * third) ** 2
    smooth_mid = 13.0 / 12.0 * (second - 2.0 * third + fourth) ** 2 + 0.25 * (second - fourth) ** 2
    smooth_right = 13.0 / 12.0 * (third - 2.0 * fourth + fifth) ** 2 + 0.25 * (3.0 * third - 4.0 * fourth + fifth) ** 2
    weight_left = 0.1 / (epsilon + smooth_left) ** 2
    weight_mid = 0.6 / (epsilon + smooth_mid) ** 2
    weight_right = 0.3 / (epsilon + smooth_right) ** 2
    return (weight_left * guess_left + weight_mid * guess_mid + weight_right * guess_right) / (weight_left + weight_mid + weight_right)

def divergence(state, metric_row, array_dim):
    cells = state.shape[array_dim] - 6
    faces = cells + 1
    density = state[0:1]
    velocity = state[1:4] / density
    speed_sq = lax.optimization_barrier(jnp.sum(velocity * velocity, axis=0, keepdims=True))
    pressure = 0.4 * (state[4:5] - 0.5 * density * speed_sq)
    contra = lax.optimization_barrier(jnp.sum(metric_row * velocity, axis=0, keepdims=True))
    metric_sq = lax.optimization_barrier(jnp.sum(metric_row * metric_row, axis=0, keepdims=True))
    wave_speed = jnp.abs(contra) + jnp.sqrt(1.4 * pressure / density * metric_sq)
    fluxes = jnp.concatenate([density * contra, state[1:4] * contra + metric_row * pressure, (state[4:5] + pressure) * contra], axis=0)
    split_plus = 0.5 * (fluxes + wave_speed * state)
    split_minus = 0.5 * (fluxes - wave_speed * state)
    inviscid = reconstruct(window(split_plus, 0, faces, array_dim), window(split_plus, 1, faces, array_dim), window(split_plus, 2, faces, array_dim), window(split_plus, 3, faces, array_dim), window(split_plus, 4, faces, array_dim))
    inviscid = inviscid + reconstruct(window(split_minus, 5, faces, array_dim), window(split_minus, 4, faces, array_dim), window(split_minus, 3, faces, array_dim), window(split_minus, 2, faces, array_dim), window(split_minus, 1, faces, array_dim))
    heat = 0.5 * speed_sq + conduction * pressure / density
    diffused = jnp.concatenate([velocity, heat], axis=0)
    face_metric = 0.5 * (window(metric_sq, 2, faces, array_dim) + window(metric_sq, 3, faces, array_dim))
    viscous = viscosity * face_metric * (window(diffused, 3, faces, array_dim) - window(diffused, 2, faces, array_dim))
    net_flux = jnp.concatenate([-inviscid[0:1], viscous - inviscid[1:5]], axis=0)
    return window(net_flux, 1, cells, array_dim) - window(net_flux, 0, cells, array_dim)

def identity_row(which):
    return jnp.eye(3, dtype=jnp.float32)[which][:, None, None, None]

def conserved(density, velocity, pressure):
    speed_sq = lax.optimization_barrier(jnp.sum(velocity * velocity, axis=0))
    return jnp.concatenate([density[None], density[None] * velocity, (pressure / 0.4 + 0.5 * density * speed_sq)[None]], axis=0)

def pad_normal(state, partner):
    wake_rows = state[:, :, 1:4, :]
    below = jnp.take(wake_rows, partner, axis=1)[:, :, ::-1, :]
    above = jnp.broadcast_to(state[:, :, -1:, :], below.shape)
    return jnp.concatenate([below, state, above], axis=2)

def span_wrap(array):
    return jnp.concatenate([array[..., -3:], array, array[..., :3]], axis=-1)

def edge_pad(array, array_dim):
    widths = [(0, 0)] * array.ndim
    widths[array_dim] = (3, 3)
    return jnp.pad(array, widths, mode='edge')

def reference(density, velocity, pressure, metrics, volume, wake_partner, iblank):
    state0 = conserved(density, velocity, pressure)
    row_chord = span_wrap(metrics[0:3] + identity_row(0))
    row_normal = span_wrap(metrics[3:6] + identity_row(1))
    row_span = span_wrap(metrics[6:9] + identity_row(2))
    mask = iblank.astype(jnp.float32)[None]
    blocks = NK // CK

    def full_rhs(state):
        wrapped = span_wrap(state)

        def block_rhs(block_id):
            start = (block_id * CK).astype(jnp.int32)
            piece = lax.dynamic_slice_in_dim(wrapped, start, CK + 6, 3)
            center = piece[..., 3:-3]
            padded_chord = edge_pad(center, 1)
            padded_normal = pad_normal(center, wake_partner)
            metric_chord = edge_pad(lax.dynamic_slice_in_dim(row_chord, start, CK + 6, 3)[..., 3:-3], 1)
            metric_normal = edge_pad(lax.dynamic_slice_in_dim(row_normal, start, CK + 6, 3)[..., 3:-3], 2)
            metric_span = lax.dynamic_slice_in_dim(row_span, start, CK + 6, 3)
            cell_volume = lax.dynamic_slice_in_dim(volume, start, CK, 2)
            total = divergence(padded_chord, metric_chord, 1) + divergence(padded_normal, metric_normal, 2) + divergence(piece, metric_span, 3)
            return total / cell_volume[None]
        stacked = lax.map(block_rhs, jnp.arange(blocks, dtype=jnp.int32))
        return jnp.transpose(stacked, (1, 2, 3, 0, 4)).reshape(5, NI, J, NK)
    state1 = state0 + time_step * mask * full_rhs(state0)
    return 0.5 * state0 + 0.5 * (state1 + time_step * mask * full_rhs(state1))
```

```python
import jax
import jax.numpy as jnp
from jax import lax
from jax.experimental import pallas as pl
from jax.experimental.pallas import tpu as pltpu
from jax.sharding import PartitionSpec as P

MESH = pl.DeviceIdType.MESH
F32 = jnp.float32
CELLS = 16
POINTS = CELLS + 6
ROWS = 256
LANES = 128
PLANE = 16
HALO = 3 * PLANE
PADDED = ROWS + 2 * HALO
KROWS = LANES + 16
TIME_STEP = 0.05


def point_terms(prims, metric, direction):
    rho, u, v, w, pressure = prims
    x = list(metric)
    x[direction] = x[direction] + 1.0
    temperature = pressure / rho
    half_sq = 0.5 * (u * u + v * v + w * w)
    contra = x[0] * u + x[1] * v + x[2] * w
    metric_sq = x[0] * x[0] + x[1] * x[1] + x[2] * x[2]
    wave = jnp.abs(contra) + jnp.sqrt(1.4 * temperature * metric_sq)
    energy = 2.5 * pressure + rho * half_sq
    mass_flux = rho * contra
    mass_wave = rho * wave
    plus, minus = [], []
    fluxes = [mass_flux] + [mass_flux * vel + x[m] * pressure for m, vel in enumerate((u, v, w))]
    fluxes.append((energy + pressure) * contra)
    spread = [mass_wave, mass_wave * u, mass_wave * v, mass_wave * w, wave * energy]
    plus = [f + s for f, s in zip(fluxes, spread)]
    minus = [f - s for f, s in zip(fluxes, spread)]
    return plus + minus + [u, v, w, half_sq + temperature, 1.6 * metric_sq]


def smoothness(before, after):
    curve = after - before
    slope = after + before
    curve4 = 4.0 * curve
    square = curve4 * curve
    middle = square * (13.0 / 12.0) + (slope * slope + 16e-6)
    sides = middle + square
    cross = curve4 * slope
    left = sides + cross
    right = sides - cross
    return curve * (1.0 / 3.0), slope, left * left, middle * middle, right * right


def blend(first, second, third, far, near):
    near_sum = third + second
    total = second * third + first * near_sum
    return second * (third * far + first * near) / total


def line_sweep(load, viscous, store):
    state = []
    for sign in range(2):
        state.append({"v": load(sign, 1), "d": None})
        state[sign]["d"] = state[sign]["v"] - load(sign, 0)
    history = [[], []]
    slopes = {}
    plus_face = {}
    face_before = None
    for p in range(1, POINTS - 1):
        for sign in range(2):
            now = state[sign]
            ahead = load(sign, p + 1)
            after = ahead - now["v"]
            curve, slope, left, middle, right = smoothness(now["d"], after)
            now["v"], now["d"] = ahead, after
            history[sign].append((curve, left, middle, right))
            if len(history[sign]) > 4:
                history[sign].pop(0)
            slopes[p] = slope if sign == 0 else slopes[p] + slope
        if p >= 3:
            face = p - 3
            if face <= CELLS:
                (c0, l0, _, _), (c1, _, m1, _), (c2, _, _, r2) = history[0][-3:]
                plus_face[face] = c1 + blend(6.0 * l0, m1, 2.0 * r2, 2.0 * (c1 - c0), c2 - c1)
        if p >= 4:
            face = p - 4
            (c2, l2, _, _), (c1, _, m1, _), (c0, _, _, r0) = history[1][-3:]
            value = plus_face.pop(face) + (
                c1 - blend(6.0 * r0, m1, 2.0 * l2, 2.0 * (c0 - c1), c1 - c2)
            )
            if viscous is not None:
                value = value + viscous(face)
            if face >= 1:
                store(face - 1, value - face_before - slopes.pop(face + 2))
            face_before = value


def kernel(
    rho_hbm, vel_hbm, prs_hbm, met_hbm, vol_hbm, blank_hbm, partner_ref, out_ref,
    prims_a, prims_b, chord, normal, span_rows, volume, blank, coef,
    wake_send_a, wake_send_b, wake_recv_a, wake_recv_b, wake_rows,
    spans_a, spans_b, span_metric, terms, net_i, net_j, net_k, half, result,
    local_sem, send_sem, recv_sem, out_sem,
):
    wrap, wraps = lax.axis_index("wrap"), lax.axis_size("wrap")
    span, spans = lax.axis_index("span"), lax.axis_size("span")
    up, down = lax.rem(span + 1, spans), lax.rem(span + spans - 1, spans)
    mirror = wraps - 1 - wrap
    has_left, has_right = wrap > 0, wrap < wraps - 1
    left = {"wrap": jnp.maximum(wrap - 1, 0)}
    right = {"wrap": jnp.minimum(wrap + 1, wraps - 1)}
    own = pl.ds(HALO, ROWS)

    loads = [
        pltpu.make_async_copy(src, dst, local_sem.at[n])
        for n, (src, dst) in enumerate(
            [
                (rho_hbm, prims_a.at[0, own]),
                (vel_hbm, prims_a.at[pl.ds(1, 3), own]),
                (prs_hbm, prims_a.at[4, own]),
                (met_hbm.at[pl.ds(6, 3)], span_rows),
                (met_hbm.at[pl.ds(0, 3)], chord.at[:, own]),
                (met_hbm.at[pl.ds(3, 3)], normal),
                (vol_hbm, volume),
                (blank_hbm, blank),
            ]
        )
    ]
    for load in loads:
        load.start()

    barrier = pltpu.get_barrier_semaphore()
    for target in ({"span": up}, {"span": down}, {"wrap": mirror}):
        pl.semaphore_signal(barrier, inc=1, device_id=target, device_id_type=MESH)

    @pl.when(has_left)
    def _():
        pl.semaphore_signal(barrier, inc=1, device_id=left, device_id_type=MESH)

    @pl.when(has_right)
    def _():
        pl.semaphore_signal(barrier, inc=1, device_id=right, device_id_type=MESH)

    pl.semaphore_wait(barrier, 3 + has_left.astype(jnp.int32) + has_right.astype(jnp.int32))

    def remote(src, dst, n, target):
        return pltpu.make_async_remote_copy(
            src_ref=src, dst_ref=dst, send_sem=send_sem.at[n], recv_sem=recv_sem.at[n],
            device_id=target, device_id_type=MESH,
        )

    first, last = pl.ds(0, HALO), pl.ds(ROWS - HALO, HALO)
    low, high = pl.ds(0, HALO), pl.ds(HALO + ROWS, HALO)
    three = pl.ds(1, 3)
    to_right_a = [
        remote(rho_hbm.at[last], prims_a.at[0, low], 0, right),
        remote(vel_hbm.at[:, last], prims_a.at[three, low], 1, right),
        remote(prs_hbm.at[last], prims_a.at[4, low], 2, right),
        remote(met_hbm.at[pl.ds(0, 3), last], chord.at[:, low], 3, right),
    ]
    to_left_a = [
        remote(rho_hbm.at[first], prims_a.at[0, high], 4, left),
        remote(vel_hbm.at[:, first], prims_a.at[three, high], 5, left),
        remote(prs_hbm.at[first], prims_a.at[4, high], 6, left),
        remote(met_hbm.at[pl.ds(0, 3), first], chord.at[:, high], 7, left),
    ]
    wake_a = remote(wake_send_a, wake_recv_a, 8, {"wrap": mirror})
    bottom, top = pl.ds(8, 8), pl.ds(LANES, 8)
    below, above = pl.ds(0, 8), pl.ds(8 + LANES, 8)
    spans_1 = [
        remote(spans_a.at[:, :, top], spans_a.at[:, :, below], 9, {"span": up}),
        remote(span_metric.at[:, :, top], span_metric.at[:, :, below], 10, {"span": up}),
        remote(spans_a.at[:, :, bottom], spans_a.at[:, :, above], 11, {"span": down}),
        remote(span_metric.at[:, :, bottom], span_metric.at[:, :, above], 12, {"span": down}),
    ]
    to_right_b = [remote(prims_b.at[:, pl.ds(ROWS, HALO)], prims_b.at[:, low], 13, right)]
    to_left_b = [remote(prims_b.at[:, pl.ds(HALO, HALO)], prims_b.at[:, high], 14, left)]
    wake_b = remote(wake_send_b, wake_recv_b, 15, {"wrap": mirror})
    spans_2 = [
        remote(spans_b.at[:, :, top], spans_b.at[:, :, below], 16, {"span": up}),
        remote(spans_b.at[:, :, bottom], spans_b.at[:, :, above], 17, {"span": down}),
    ]

    def start_sides(to_left, to_right):
        @pl.when(has_right)
        def _():
            for copy in to_right:
                copy.start()

        @pl.when(has_left)
        def _():
            for copy in to_left:
                copy.start()

    def finish_sides(to_left, to_right, arrays):
        @pl.when(has_left)
        def _():
            for copy in to_right:
                copy.wait_recv()

        @pl.when(has_right)
        def _():
            for copy in to_left:
                copy.wait_recv()

        @pl.when(jnp.logical_not(has_left))
        def _():
            for array, count in arrays:
                for m in range(count):
                    edge = array[m, HALO : HALO + PLANE, :]
                    for n in range(3):
                        array[m, n * PLANE : (n + 1) * PLANE, :] = edge

        @pl.when(jnp.logical_not(has_right))
        def _():
            for array, count in arrays:
                for m in range(count):
                    edge = array[m, HALO + ROWS - PLANE : HALO + ROWS, :]
                    for n in range(3):
                        start = HALO + ROWS + n * PLANE
                        array[m, start : start + PLANE, :] = edge

    def drain_sides(to_left, to_right):
        @pl.when(has_right)
        def _():
            for copy in to_right:
                copy.wait_send()

        @pl.when(has_left)
        def _():
            for copy in to_left:
                copy.wait_send()

    def pack_wake(prims, send):
        flat_send = send.reshape(ROWS, LANES)
        for m in range(5):
            for r in range(3):
                for h in range(2):
                    rows = prims[m, pl.ds(HALO + 128 * h + 1 + r, 8, stride=16), :]
                    flat_send[pl.ds(128 * h + 3 * m + r, 8, stride=16), :] = rows

    def unpack_wake(recv):
        slab = mirror * CELLS
        for i in range(CELLS):
            wake_rows[i * 16 : (i + 1) * 16, :] = recv[jnp.clip(partner_ref[i] - slab, 0, CELLS - 1)]

    def turn(src, dst, count, base):
        def body(n, carry):
            m, t = n // 2, lax.rem(n, 2)
            start = pl.multiple_of(base + 128 * t, 16)
            dst[m, t, 8 : 8 + LANES, :] = src[m, pl.ds(start, LANES), :].T
            return carry

        lax.fori_loop(0, 2 * count, body, 0)

    def put_terms(direction, p, h, values):
        for f, value in enumerate(values):
            terms[direction, f, 2 * p + h] = value

    def points_i(prims, begin, end):
        def body(p, carry):
            for h in range(2):
                rows = pl.ds(pl.multiple_of(p * PLANE + 8 * h, 8), 8)
                values = point_terms(
                    [prims[m, rows, :] for m in range(5)], [chord[m, rows, :] for m in range(3)], 0
                )
                put_terms(0, p, h, values)
            return carry

        lax.fori_loop(begin, end, body, 0)

    def points_j(prims, begin, end):
        def body(p, carry):
            for h in range(2):
                j = jnp.clip(p - 3, 0, CELLS - 1)
                rows = pl.ds(HALO + 128 * h + j, 8, stride=16)
                metric_rows = pl.ds(128 * h + j, 8, stride=16)
                values = point_terms(
                    [prims[m, rows, :] for m in range(5)],
                    [normal[m, metric_rows, :] for m in range(3)],
                    1,
                )
                put_terms(1, p, h, values)
            return carry

        lax.fori_loop(begin, end, body, 0)

    def points_wake():
        for p in range(3):
            for h in range(2):
                values = point_terms(
                    [wake_rows[pl.ds(128 * h + 3 * m + 2 - p, 8, stride=16), :] for m in range(5)],
                    [normal[m, pl.ds(128 * h, 8, stride=16), :] for m in range(3)],
                    1,
                )
                put_terms(1, p, h, values)

    def points_k(array):
        def body(p, carry):
            for h in range(2):
                rows = pl.ds(5 + p, 8, stride=16)
                values = point_terms(
                    [array[m, h, rows, :] for m in range(5)],
                    [span_metric[m, h, rows, :] for m in range(3)],
                    2,
                )
                put_terms(2, p, h, values)
            return carry

        lax.fori_loop(0, POINTS, body, 0)

    def sweep(direction, put):
        def one(m, h, with_viscous):
            def load(sign, p):
                return terms[direction, 5 * sign + m, 2 * p + h]

            def viscous(face):
                a, b = 2 * (face + 2) + h, 2 * (face + 3) + h
                scale = terms[direction, 14, a] + terms[direction, 14, b]
                return scale * (terms[direction, 9 + m, b] - terms[direction, 9 + m, a])

            line_sweep(load, viscous if with_viscous else None, lambda n, v: put(m, h, n, v))

        def mass(h, carry):
            one(0, h, False)
            return carry

        def others(n, carry):
            one(1 + n // 2, lax.rem(n, 2), True)
            return carry

        lax.fori_loop(0, 2, mass, 0)
        lax.fori_loop(0, 8, others, 0)

    def put_i(m, h, n, value):
        net_i[m, pl.ds(pl.multiple_of(n * PLANE + 8 * h, 8), 8), :] = value

    def put_j(m, h, n, value):
        net_j[m, pl.ds(128 * h + n, 8, stride=16), :] = value

    def put_k(m, h, n, value):
        net_k[m, h, pl.ds(n, 8, stride=16), :] = value

    def turn_back():
        def body(n, carry):
            m, t = n // 2, lax.rem(n, 2)
            rows = pl.ds(pl.multiple_of(128 * t, 128), LANES)
            net_i[m, rows, :] = net_i[m, rows, :] + net_j[m, rows, :] + net_k[m, t].T
            return carry

        lax.fori_loop(0, 10, body, 0)

    def update_first(n, carry):
        rows = pl.ds(pl.multiple_of(8 * n, 8), 8)
        at = pl.ds(pl.multiple_of(HALO + 8 * n, 8), 8)
        rho, u, v, w, pressure = [prims_a[m, at, :] for m in range(5)]
        scale = coef[rows, :]
        energy = 2.5 * pressure + 0.5 * rho * (u * u + v * v + w * w)
        before = [rho, rho * u, rho * v, rho * w, energy]
        after = [b + scale * net_i[m, rows, :] for m, b in enumerate(before)]
        for m in range(5):
            half[m, rows, :] = 0.5 * (before[m] + after[m])
        vel = [after[m] / after[0] for m in (1, 2, 3)]
        speed_sq = vel[0] * vel[0] + vel[1] * vel[1] + vel[2] * vel[2]
        prims_b[0, at, :] = after[0]
        for m in range(3):
            prims_b[1 + m, at, :] = vel[m]
        prims_b[4, at, :] = 0.4 * (after[4] - 0.5 * after[0] * speed_sq)
        return carry

    def update_second(n, carry):
        rows = pl.ds(pl.multiple_of(8 * n, 8), 8)
        scale = 0.5 * coef[rows, :]
        for m in range(5):
            result[m, rows, :] = half[m, rows, :] + scale * net_i[m, rows, :]
        return carry

    start_sides(to_left_a, to_right_a)
    for load in loads[:4]:
        load.wait()
    pack_wake(prims_a, wake_send_a)
    wake_a.start()
    turn(prims_a, spans_a, 5, HALO)
    turn(span_rows, span_metric, 3, 0)
    for copy in spans_1:
        copy.start()
    for load in loads[4:]:
        load.wait()

    def scale_rows(n, carry):
        rows = pl.ds(pl.multiple_of(8 * n, 8), 8)
        coef[rows, :] = (0.25 * TIME_STEP) * blank[rows, :].astype(F32) / volume[rows, :]
        return carry

    lax.fori_loop(0, ROWS // 8, scale_rows, 0)

    def stage(prims, array, span_copies, to_left, to_right, edges, wake, recv):
        points_i(prims, 3, 3 + CELLS)
        points_j(prims, 3, POINTS)
        for copy in span_copies:
            copy.wait_recv()
        points_k(array)
        sweep(2, put_k)
        finish_sides(to_left, to_right, edges)
        points_i(prims, 0, 3)
        points_i(prims, 3 + CELLS, POINTS)
        sweep(0, put_i)
        wake.wait_recv()
        unpack_wake(recv)
        points_wake()
        sweep(1, put_j)
        turn_back()
        drain_sides(to_left, to_right)
        for copy in span_copies:
            copy.wait_send()
        wake.wait_send()

    stage(
        prims_a, spans_a, spans_1, to_left_a, to_right_a,
        [(prims_a, 5), (chord, 3)], wake_a, wake_recv_a,
    )
    lax.fori_loop(0, ROWS // 8, update_first, 0)
    start_sides(to_left_b, to_right_b)
    pack_wake(prims_b, wake_send_b)
    wake_b.start()
    turn(prims_b, spans_b, 5, HALO)
    for copy in spans_2:
        copy.start()
    stage(
        prims_b, spans_b, spans_2, to_left_b, to_right_b,
        [(prims_b, 5)], wake_b, wake_recv_b,
    )
    lax.fori_loop(0, ROWS // 8, update_second, 0)
    done = pltpu.make_async_copy(result, out_ref, out_sem)
    done.start()
    done.wait()


def body(density, velocity, pressure, metrics, volume, wake_partner, iblank):
    flat = lambda array: array.reshape(array.shape[:-3] + (ROWS, LANES))
    anywhere = pl.BlockSpec(memory_space=pl.ANY)
    out = pl.pallas_call(
        kernel,
        out_shape=jax.ShapeDtypeStruct((5, ROWS, LANES), F32),
        in_specs=[anywhere] * 6 + [pl.BlockSpec(memory_space=pltpu.SMEM)],
        out_specs=anywhere,
        scratch_shapes=[
            pltpu.VMEM((5, PADDED, LANES), F32),
            pltpu.VMEM((5, PADDED, LANES), F32),
            pltpu.VMEM((3, PADDED, LANES), F32),
            pltpu.VMEM((3, ROWS, LANES), F32),
            pltpu.VMEM((3, ROWS, LANES), F32),
            pltpu.VMEM((ROWS, LANES), F32),
            pltpu.VMEM((ROWS, LANES), jnp.int32),
            pltpu.VMEM((ROWS, LANES), F32),
            pltpu.VMEM((CELLS, 16, LANES), F32),
            pltpu.VMEM((CELLS, 16, LANES), F32),
            pltpu.VMEM((CELLS, 16, LANES), F32),
            pltpu.VMEM((CELLS, 16, LANES), F32),
            pltpu.VMEM((ROWS, LANES), F32),
            pltpu.VMEM((5, 2, KROWS, LANES), F32),
            pltpu.VMEM((5, 2, KROWS, LANES), F32),
            pltpu.VMEM((3, 2, KROWS, LANES), F32),
            pltpu.VMEM((3, 15, 2 * POINTS, 8, LANES), F32),
            pltpu.VMEM((5, ROWS, LANES), F32),
            pltpu.VMEM((5, ROWS, LANES), F32),
            pltpu.VMEM((5, 2, LANES, LANES), F32),
            pltpu.VMEM((5, ROWS, LANES), F32),
            pltpu.VMEM((5, ROWS, LANES), F32),
            pltpu.SemaphoreType.DMA((8,)),
            pltpu.SemaphoreType.DMA((18,)),
            pltpu.SemaphoreType.DMA((18,)),
            pltpu.SemaphoreType.DMA,
        ],
        compiler_params=pltpu.CompilerParams(
            collective_id=0, has_side_effects=True, vmem_limit_bytes=63 * 1024 * 1024
        ),
        name="weno_sections",
    )(
        flat(density), flat(velocity), flat(pressure), flat(metrics), flat(volume),
        flat(iblank), wake_partner,
    )
    return out.reshape(5, CELLS, PLANE, LANES)


def solution(mesh):
    placed = (
        P("wrap", None, "span"),
        P(None, "wrap", None, "span"),
        P("wrap", None, "span"),
        P(None, "wrap", None, "span"),
        P("wrap", None, "span"),
        P("wrap"),
        P("wrap", None, "span"),
    )
    return jax.shard_map(
        body, mesh=mesh, in_specs=placed, out_specs=P(None, "wrap", None, "span"), check_vma=False
    )
```

```python
import jax
import jax.numpy as jnp
from jax import lax
from jax.experimental import pallas as pl
from jax.experimental.pallas import tpu as pltpu
from jax.sharding import PartitionSpec as P

MESH = pl.DeviceIdType.MESH
F32 = jnp.float32
CELLS = 16
POINTS = CELLS + 6
ROWS = 256
LANES = 128
PLANE = 16
HALO = 3 * PLANE
PADDED = ROWS + 2 * HALO
ODD = PLANE + 1
SPAN_ROWS = 176
TIME_STEP = 0.05


def point_terms(prims, metric, direction):
    rho, u, v, w, pressure = prims
    x = list(metric)
    x[direction] = x[direction] + 1.0
    temperature = pressure / rho
    half_sq = 0.5 * (u * u + v * v + w * w)
    contra = x[0] * u + x[1] * v + x[2] * w
    metric_sq = x[0] * x[0] + x[1] * x[1] + x[2] * x[2]
    wave = jnp.abs(contra) + jnp.sqrt(1.4 * temperature * metric_sq)
    energy = 2.5 * pressure + rho * half_sq
    mass_flux = rho * contra
    mass_wave = rho * wave
    fluxes = [mass_flux] + [mass_flux * vel + x[m] * pressure for m, vel in enumerate((u, v, w))]
    fluxes.append((energy + pressure) * contra)
    spread = [mass_wave, mass_wave * u, mass_wave * v, mass_wave * w, wave * energy]
    plus = [f + s for f, s in zip(fluxes, spread)]
    minus = [f - s for f, s in zip(fluxes, spread)]
    whole = [6.0 * f for f in fluxes]
    return plus + minus + whole + [u, v, w, half_sq + temperature, 4.8 * metric_sq]


def smoothness(before, after):
    curve = after - before
    base = curve * curve * (4.0 / 3.0) + 4e-6
    left = base + after * (after + curve)
    middle = base + after * before
    right = base + before * (before - curve)
    return curve, left * left, middle * middle, right * right


def blend(first, second, third, far, near):
    near_sum = third + second
    total = second * third + first * near_sum
    return second * (third * far + first * near) / total


def line_sweep(load, whole, viscous, store, begin, end):
    state = []
    for sign in range(2):
        value = load(sign, begin + 1)
        state.append([value, value - load(sign, begin)])
    history = [[], []]
    plus_face = {}
    face_before = None
    for p in range(begin + 1, end + 5):
        for sign in range(2):
            value, before = state[sign]
            ahead = load(sign, p + 1)
            after = ahead - value
            history[sign].append(smoothness(before, after))
            state[sign] = [ahead, after]
            if len(history[sign]) > 3:
                history[sign].pop(0)
        face = p - 3
        if begin <= face <= end:
            (c0, l0, _, _), (c1, _, m1, _), (c2, _, _, r2) = history[0]
            plus_face[face] = c1 + blend(6.0 * l0, m1, 2.0 * r2, 2.0 * (c1 - c0), c2 - c1)
        face = p - 4
        if face >= begin:
            (c2, l2, _, _), (c1, _, m1, _), (c0, _, _, r0) = history[1]
            value = plus_face.pop(face) + (
                c1 - blend(6.0 * r0, m1, 2.0 * l2, 2.0 * (c0 - c1), c1 - c2)
            )
            if viscous is not None:
                value = value + viscous(face)
            if face > begin:
                n = face - 1
                store(n, value - face_before - (whole(n + 4) - whole(n + 2)))
            face_before = value


def kernel(
    rho_hbm, vel_hbm, prs_hbm, met_hbm, vol_hbm, blank_hbm, partner_ref, result,
    prims_a, prims_b, prims_j, chord, normal, normal_j, span_rows, volume, blank, coef,
    wake_send_a, wake_send_b, wake_recv_a, wake_recv_b, wake_rows,
    spans, span_metric, pack_up_a, pack_down_a, pack_up_b, pack_down_b,
    below_a, above_a, below_b, above_b,
    terms, net_i, net_j, net_k, turned, half,
    local_sem, send_sem, recv_sem,
):
    wrap, wraps = lax.axis_index("wrap"), lax.axis_size("wrap")
    span, span_count = lax.axis_index("span"), lax.axis_size("span")
    up, down = lax.rem(span + 1, span_count), lax.rem(span + span_count - 1, span_count)
    mirror = wraps - 1 - wrap
    has_left, has_right = wrap > 0, wrap < wraps - 1
    left = {"wrap": jnp.maximum(wrap - 1, 0)}
    right = {"wrap": jnp.minimum(wrap + 1, wraps - 1)}
    own = pl.ds(HALO, ROWS)

    loads = [
        pltpu.make_async_copy(src, dst, local_sem.at[n])
        for n, (src, dst) in enumerate(
            [
                (rho_hbm, prims_a.at[0, own]),
                (vel_hbm, prims_a.at[pl.ds(1, 3), own]),
                (prs_hbm, prims_a.at[4, own]),
                (met_hbm.at[pl.ds(6, 3)], span_rows),
                (met_hbm.at[pl.ds(3, 3)], normal),
                (met_hbm.at[pl.ds(0, 3)], chord.at[:, own]),
                (vol_hbm, volume),
                (blank_hbm, blank),
            ]
        )
    ]
    for load in loads:
        load.start()

    barrier = pltpu.get_barrier_semaphore()
    for target in ({"span": up}, {"span": down}, {"wrap": mirror}):
        pl.semaphore_signal(barrier, inc=1, device_id=target, device_id_type=MESH)

    @pl.when(has_left)
    def _():
        pl.semaphore_signal(barrier, inc=1, device_id=left, device_id_type=MESH)

    @pl.when(has_right)
    def _():
        pl.semaphore_signal(barrier, inc=1, device_id=right, device_id_type=MESH)

    def remote(src, dst, n, target):
        return pltpu.make_async_remote_copy(
            src_ref=src, dst_ref=dst, send_sem=send_sem.at[n], recv_sem=recv_sem.at[n],
            device_id=target, device_id_type=MESH,
        )

    first, last = pl.ds(0, HALO), pl.ds(ROWS - HALO, HALO)
    low, high = pl.ds(0, HALO), pl.ds(HALO + ROWS, HALO)
    three = pl.ds(1, 3)
    to_right_a = [
        remote(rho_hbm.at[last], prims_a.at[0, low], 0, right),
        remote(vel_hbm.at[:, last], prims_a.at[three, low], 1, right),
        remote(prs_hbm.at[last], prims_a.at[4, low], 2, right),
        remote(met_hbm.at[pl.ds(0, 3), last], chord.at[:, low], 3, right),
    ]
    to_left_a = [
        remote(rho_hbm.at[first], prims_a.at[0, high], 4, left),
        remote(vel_hbm.at[:, first], prims_a.at[three, high], 5, left),
        remote(prs_hbm.at[first], prims_a.at[4, high], 6, left),
        remote(met_hbm.at[pl.ds(0, 3), first], chord.at[:, high], 7, left),
    ]
    wake_a = remote(wake_send_a, wake_recv_a, 8, {"wrap": mirror})
    spans_1 = [
        remote(pack_up_a, below_a, 9, {"span": up}),
        remote(pack_down_a, above_a, 10, {"span": down}),
    ]
    to_right_b = [remote(prims_b.at[:, pl.ds(ROWS, HALO)], prims_b.at[:, low], 11, right)]
    to_left_b = [remote(prims_b.at[:, pl.ds(HALO, HALO)], prims_b.at[:, high], 12, left)]
    wake_b = remote(wake_send_b, wake_recv_b, 13, {"wrap": mirror})
    spans_2 = [
        remote(pack_up_b, below_b, 14, {"span": up}),
        remote(pack_down_b, above_b, 15, {"span": down}),
    ]

    def start_sides(to_left, to_right):
        @pl.when(has_right)
        def _():
            for copy in to_right:
                copy.start()

        @pl.when(has_left)
        def _():
            for copy in to_left:
                copy.start()

    def finish_sides(to_left, to_right, arrays):
        @pl.when(has_left)
        def _():
            for copy in to_right:
                copy.wait_recv()

        @pl.when(has_right)
        def _():
            for copy in to_left:
                copy.wait_recv()

        @pl.when(jnp.logical_not(has_left))
        def _():
            for array, count in arrays:
                for m in range(count):
                    edge = array[m, HALO : HALO + PLANE, :]
                    for n in range(3):
                        array[m, n * PLANE : (n + 1) * PLANE, :] = edge

        @pl.when(jnp.logical_not(has_right))
        def _():
            for array, count in arrays:
                for m in range(count):
                    edge = array[m, HALO + ROWS - PLANE : HALO + ROWS, :]
                    for n in range(3):
                        start = HALO + ROWS + n * PLANE
                        array[m, start : start + PLANE, :] = edge

    def drain_sides(to_left, to_right):
        @pl.when(has_right)
        def _():
            for copy in to_right:
                copy.wait_send()

        @pl.when(has_left)
        def _():
            for copy in to_left:
                copy.wait_send()

    def spread_rows(src, base, dst, count):
        for m in range(count):
            for i in range(CELLS):
                rows = src[m, base + PLANE * i : base + PLANE * (i + 1), :]
                dst[m, ODD * i : ODD * i + PLANE, :] = rows

    def pack_wake(prims, send):
        for i in range(CELLS):
            for m in range(5):
                start = HALO + PLANE * i + 1
                send[i, 3 * m : 3 * m + 3, :] = prims[m, start : start + 3, :]

    def unpack_wake(recv):
        slab = mirror * CELLS
        for i in range(CELLS):
            rows = recv[jnp.clip(partner_ref[i] - slab, 0, CELLS - 1)]
            wake_rows[ODD * i : ODD * i + PLANE, :] = rows

    def turn(src, dst, count, base):
        for m in range(count):
            for t in range(2):
                block = src[m, base + LANES * t : base + LANES * (t + 1), :].T
                for q in range(8):
                    start = ODD * (q + 1)
                    dst[m, t, start : start + CELLS, :] = block[CELLS * q : CELLS * (q + 1), :]

    def pack_spans(arrays, pack_up, pack_down):
        n = 0
        for array, count in arrays:
            for m in range(count):
                for t in range(2):
                    pack_up[n : n + 3, :] = array[m, t, 8 * ODD + 13 : 8 * ODD + 16, :]
                    pack_down[n : n + 3, :] = array[m, t, ODD : ODD + 3, :]
                    n += 3

    def unpack_spans(arrays, below, above):
        n = 0
        for array, count in arrays:
            for m in range(count):
                for t in range(2):
                    array[m, t, 13:16, :] = below[n : n + 3, :]
                    array[m, t, 9 * ODD : 9 * ODD + 3, :] = above[n : n + 3, :]
                    n += 3

    def put_terms(direction, p, h, values):
        for f, value in enumerate(values):
            terms[direction, f, 2 * p + h] = value

    def points_i(prims, begin, end, unroll):
        def body(p, carry):
            for h in range(2):
                rows = pl.ds(pl.multiple_of(p * PLANE + 8 * h, 8), 8)
                values = point_terms(
                    [prims[m, rows, :] for m in range(5)], [chord[m, rows, :] for m in range(3)], 0
                )
                put_terms(0, p, h, values)
            return carry

        lax.fori_loop(begin, end, body, 0, unroll=unroll)

    def points_j():
        def at(j, h):
            rows = pl.ds(ODD * 8 * h + j, 8, stride=ODD)
            return point_terms(
                [prims_j[m, rows, :] for m in range(5)], [normal_j[m, rows, :] for m in range(3)], 1
            )

        def body(j, carry):
            for h in range(2):
                put_terms(1, j + 3, h, at(j, h))
            return carry

        lax.fori_loop(0, CELLS - 2, body, 0, unroll=2)
        for h in range(2):
            put_terms(1, CELLS + 1, h, at(CELLS - 2, h))
            values = at(CELLS - 1, h)
            for p in range(CELLS + 2, POINTS):
                put_terms(1, p, h, values)

    def points_wake():
        for p in range(3):
            for h in range(2):
                values = point_terms(
                    [
                        wake_rows[pl.ds(ODD * 8 * h + 3 * m + 2 - p, 8, stride=ODD), :]
                        for m in range(5)
                    ],
                    [normal_j[m, pl.ds(ODD * 8 * h, 8, stride=ODD), :] for m in range(3)],
                    1,
                )
                put_terms(1, p, h, values)

    def points_k(begin, end, shift, unroll):
        def body(p, carry):
            for h in range(2):
                rows = pl.ds(p + shift, 8, stride=ODD)
                values = point_terms(
                    [spans[m, h, rows, :] for m in range(5)],
                    [span_metric[m, h, rows, :] for m in range(3)],
                    2,
                )
                put_terms(2, p, h, values)
            return carry

        lax.fori_loop(begin, end, body, 0, unroll=unroll)

    def sweep(direction, put, begin=0, end=CELLS):
        def one(m, h, with_viscous):
            def load(sign, p):
                return terms[direction, 5 * sign + m, 2 * p + h]

            def whole(p):
                return terms[direction, 10 + m, 2 * p + h]

            def viscous(face):
                a, b = 2 * (face + 2) + h, 2 * (face + 3) + h
                scale = terms[direction, 19, a] + terms[direction, 19, b]
                return scale * (terms[direction, 14 + m, b] - terms[direction, 14 + m, a])

            line_sweep(
                load, whole, viscous if with_viscous else None,
                lambda n, v: put(m, h, n, v), begin, end,
            )

        def mass(h, carry):
            one(0, h, False)
            return carry

        def others(n, carry):
            one(1 + n // 2, lax.rem(n, 2), True)
            return carry

        lax.fori_loop(0, 2, mass, 0)
        lax.fori_loop(0, 8, others, 0)

    def put_i(m, h, n, value):
        net_i[m, pl.ds(pl.multiple_of(n * PLANE + 8 * h, 8), 8), :] = value

    def put_j(m, h, n, value):
        net_j[m, pl.ds(ODD * 8 * h + n, 8, stride=ODD), :] = value

    def put_k(m, h, n, value):
        net_k[m, h, pl.ds(n, 8, stride=ODD), :] = value

    def turn_back():
        for m in range(5):
            for t in range(2):
                parts = [net_k[m, t, ODD * q : ODD * q + CELLS, :] for q in range(8)]
                turned[m, LANES * t : LANES * (t + 1), :] = jnp.concatenate(parts, axis=0).T

    def whole_net(m, i, h, rows):
        return net_i[m, rows, :] + net_j[m, pl.ds(ODD * i + 8 * h, 8), :] + turned[m, rows, :]

    def update_first(i, carry):
        for h in range(2):
            rows = pl.ds(pl.multiple_of(PLANE * i + 8 * h, 8), 8)
            at = pl.ds(pl.multiple_of(HALO + PLANE * i + 8 * h, 8), 8)
            at_j = pl.ds(ODD * i + 8 * h, 8)
            rho, u, v, w, pressure = [prims_a[m, at, :] for m in range(5)]
            scale = coef[rows, :]
            energy = 2.5 * pressure + 0.5 * rho * (u * u + v * v + w * w)
            before = [rho, rho * u, rho * v, rho * w, energy]
            after = [b + scale * whole_net(m, i, h, rows) for m, b in enumerate(before)]
            for m in range(5):
                half[m, rows, :] = 0.5 * (before[m] + after[m])
            vel = [after[m] / after[0] for m in (1, 2, 3)]
            speed_sq = vel[0] * vel[0] + vel[1] * vel[1] + vel[2] * vel[2]
            pressure = 0.4 * (after[4] - 0.5 * after[0] * speed_sq)
            for m, value in enumerate([after[0], *vel, pressure]):
                prims_b[m, at, :] = value
                prims_j[m, at_j, :] = value
        return carry

    def update_second(i, carry):
        for h in range(2):
            rows = pl.ds(pl.multiple_of(PLANE * i + 8 * h, 8), 8)
            scale = 0.5 * coef[rows, :]
            for m in range(5):
                result[m, rows, :] = half[m, rows, :] + scale * whole_net(m, i, h, rows)
        return carry

    def scale_rows(n, carry):
        rows = pl.ds(pl.multiple_of(8 * n, 8), 8)
        coef[rows, :] = (TIME_STEP / 12.0) * blank[rows, :].astype(F32) / volume[rows, :]
        return carry

    def stage(prims, copies, arrays, received, to_left, to_right, edges, wake, recv):
        sweep(1, put_j, 3, CELLS)
        for copy in copies:
            copy.wait_recv()
        wake.start()
        unpack_spans(arrays, *received)
        points_k(0, 3, 13, 3)
        points_k(3, 3 + CELLS, 14, 2)
        points_k(3 + CELLS, POINTS, 15, 3)
        sweep(2, put_k)
        finish_sides(to_left, to_right, edges)
        points_i(prims, 0, 3, 3)
        points_i(prims, 3 + CELLS, POINTS, 3)
        sweep(0, put_i)
        wake.wait_recv()
        unpack_wake(recv)
        points_wake()
        sweep(1, put_j, 0, 3)
        turn_back()
        drain_sides(to_left, to_right)
        for copy in copies:
            copy.wait_send()
        wake.wait_send()

    for load in loads[:4]:
        load.wait()
    turn(prims_a, spans, 5, HALO)
    turn(span_rows, span_metric, 3, 0)
    both = [(spans, 5), (span_metric, 3)]
    pack_spans(both, pack_up_a, pack_down_a)
    pl.semaphore_wait(barrier, 3 + has_left.astype(jnp.int32) + has_right.astype(jnp.int32))
    for copy in spans_1:
        copy.start()
    start_sides(to_left_a, to_right_a)
    for load in loads[4:]:
        load.wait()
    pack_wake(prims_a, wake_send_a)
    spread_rows(prims_a, HALO, prims_j, 5)
    spread_rows(normal, 0, normal_j, 3)
    lax.fori_loop(0, ROWS // 8, scale_rows, 0, unroll=4)
    points_j()
    points_i(prims_a, 3, 3 + CELLS, 2)
    stage(
        prims_a, spans_1, both, (below_a, above_a), to_left_a, to_right_a,
        [(prims_a, 5), (chord, 3)], wake_a, wake_recv_a,
    )
    lax.fori_loop(0, CELLS, update_first, 0)
    turn(prims_b, spans, 5, HALO)
    pack_spans([(spans, 5)], pack_up_b, pack_down_b)
    for copy in spans_2:
        copy.start()
    start_sides(to_left_b, to_right_b)
    pack_wake(prims_b, wake_send_b)
    points_j()
    points_i(prims_b, 3, 3 + CELLS, 2)
    stage(
        prims_b, spans_2, [(spans, 5)], (below_b, above_b), to_left_b, to_right_b,
        [(prims_b, 5)], wake_b, wake_recv_b,
    )
    lax.fori_loop(0, CELLS, update_second, 0, unroll=2)


def body(density, velocity, pressure, metrics, volume, wake_partner, iblank):
    flat = lambda array: array.reshape(array.shape[:-3] + (ROWS, LANES))
    memory = lambda *shape: pltpu.VMEM(shape, F32)
    anywhere = pl.BlockSpec(memory_space=pl.ANY)
    out = pl.pallas_call(
        kernel,
        out_shape=jax.ShapeDtypeStruct((5, ROWS, LANES), F32),
        in_specs=[anywhere] * 6 + [pl.BlockSpec(memory_space=pltpu.SMEM)],
        out_specs=pl.BlockSpec(memory_space=pltpu.VMEM),
        scratch_shapes=[
            memory(5, PADDED, LANES),
            memory(5, PADDED, LANES),
            memory(5, ODD * CELLS, LANES),
            memory(3, PADDED, LANES),
            memory(3, ROWS, LANES),
            memory(3, ODD * CELLS, LANES),
            memory(3, ROWS, LANES),
            memory(ROWS, LANES),
            pltpu.VMEM((ROWS, LANES), jnp.int32),
            memory(ROWS, LANES),
            memory(CELLS, PLANE, LANES),
            memory(CELLS, PLANE, LANES),
            memory(CELLS, PLANE, LANES),
            memory(CELLS, PLANE, LANES),
            memory(ODD * CELLS, LANES),
            memory(5, 2, SPAN_ROWS, LANES),
            memory(3, 2, SPAN_ROWS, LANES),
            memory(48, LANES),
            memory(48, LANES),
            memory(32, LANES),
            memory(32, LANES),
            memory(48, LANES),
            memory(48, LANES),
            memory(32, LANES),
            memory(32, LANES),
            memory(3, 20, 2 * POINTS, 8, LANES),
            memory(5, ROWS, LANES),
            memory(5, ODD * CELLS, LANES),
            memory(5, 2, ODD * 8, LANES),
            memory(5, ROWS, LANES),
            memory(5, ROWS, LANES),
            pltpu.SemaphoreType.DMA((8,)),
            pltpu.SemaphoreType.DMA((16,)),
            pltpu.SemaphoreType.DMA((16,)),
        ],
        compiler_params=pltpu.CompilerParams(
            collective_id=0, has_side_effects=True, vmem_limit_bytes=60 * 1024 * 1024
        ),
        name="weno_sections",
    )(
        flat(density), flat(velocity), flat(pressure), flat(metrics), flat(volume),
        flat(iblank), wake_partner,
    )
    return out.reshape(5, CELLS, PLANE, LANES)


def solution(mesh):
    placed = (
        P("wrap", None, "span"),
        P(None, "wrap", None, "span"),
        P("wrap", None, "span"),
        P(None, "wrap", None, "span"),
        P("wrap", None, "span"),
        P("wrap"),
        P("wrap", None, "span"),
    )
    return jax.shard_map(
        body, mesh=mesh, in_specs=placed, out_specs=P(None, "wrap", None, "span"), check_vma=False
    )
```
